32 devices in a mesh: mesh: 8 (over y, x, core), band: 4 (over z).
Axes of the slice: x: 2, y: 2, z: 4, core: 2. Of those that a mesh axis runs over, the one named last changes fastest.
Arguments:
- orbitals: bfloat16 [8, 512, 2048], P('mesh', None, 'band'), may hold values from -6 to 6
- element_matrix: bfloat16 [8, 512, 512], P('mesh'), may hold values from -0.25 to 0.25
- face_map: int32 [8, 64], P('mesh'), may hold values from 0 to 63, as said below
- panel_order: int32 [4], replicated, may hold values from 0 to 15, as said below
Outputs:
- filtered: bfloat16 [8, 512, 2048], P('mesh', None, 'band')
- margin: float32 [2048, 512], P('band')
The draws below stay inside these ranges and needn't reach their ends.
Inputs may be any that keep to these rules, and one draw needn't show every extreme that they name: `face_map`: each row is a permutation of 0 to 63. `panel_order`: the entries are distinct; the last panel, 2048 // 128 - 1, is always among them.
All inputs are finite; a program needn't handle non-finite values.
Results may differ from the reference program's by a relative error of at most 0.0045.
Values may be sent and summed in bfloat16 or wider, within the bound.
A program may use at most 64 MiB of HBM per device.

```python
import jax
import jax.numpy as jnp
from jax import lax

ORB_DEV = 512
FACE = 64
NODES_EL = 512
PANEL = 128
PANELS = 4
ELEMENTS = 8
ORBITALS = 2048


def draw_face_map(key, part):
    keys = jax.random.split(jax.random.fold_in(key, 11), ELEMENTS)

    def one_row(row_key):
        return jax.random.permutation(row_key, FACE)
    return jax.vmap(one_row)(keys).astype(jnp.int32)


def draw_panel_order(key, part):
    first_key = jax.random.fold_in(key, 21)
    second_key = jax.random.fold_in(key, 22)
    total = ORBITALS // PANEL
    others = jax.random.permutation(first_key, total - 1)[:PANELS - 1]
    values = jnp.concatenate([others.astype(jnp.int32), jnp.array([total - 1], dtype=jnp.int32)])
    return jax.random.permutation(second_key, values).astype(jnp.int32)


def level_of(key, extent, pieces, low, top_value):
    factor_of, own = 1.0, jax.random.fold_in(key, 6)
    for position, blocks in pieces:
        steps = jnp.exp(jax.random.uniform(jax.random.fold_in(own, position), (blocks,), jnp.float32, low / len(pieces), top_value / len(pieces)))
        factor_of = factor_of * jnp.repeat(steps, extent[position] // blocks).reshape([-1 if axis == position else 1 for axis in range(len(extent))])
    return factor_of


def scatter_about(key, shape, deviation, limit, cuts=(), held_as=jnp.bfloat16):
    values = deviation * jax.random.normal(key, shape, jnp.float32)
    if cuts:
        values = values * level_of(key, shape, cuts, -0.22, 0.18)
    return jnp.clip(values, -limit, limit).astype(held_as)


def setup_inputs(seed: int = 0) -> dict:
    key_of = jax.random.split(jax.random.key(seed), 5)
    orbitals = scatter_about(key_of[0], (ELEMENTS, NODES_EL, ORBITALS), 1.0, 6.0, ((0, 8), (2, 4)))
    element_matrix = scatter_about(key_of[1], (ELEMENTS, NODES_EL, NODES_EL), NODES_EL ** -0.5, 0.25, ((0, 8),))
    face_map = draw_face_map(jax.random.fold_in(key_of[4], 71), 0)
    panel_order = draw_panel_order(jax.random.fold_in(key_of[4], 71), 0)
    return {"orbitals": orbitals, "element_matrix": element_matrix, "face_map": face_map, "panel_order": panel_order}


center_value = 0.5
half_width = 2.0


def assemble(partial_value, one_hot):
    top_face = partial_value[:, -1]
    low_face = partial_value[:, 0]
    upper_next = jnp.roll(low_face, -1, axis=0)
    summed = top_face + jnp.einsum('gfj,gjo->gfo', one_hot, upper_next, precision=lax.Precision.HIGHEST)
    moved_top = jnp.einsum('gfj,gfo->gjo', one_hot, top_face, precision=lax.Precision.HIGHEST)
    lower_new = low_face + jnp.roll(moved_top, 1, axis=0)
    return partial_value.at[:, 0].set(lower_new).at[:, -1].set(summed)


def operate(matrices, one_hot, values):
    partial_value = jnp.einsum('enm,emo->eno', matrices, values.astype(jnp.float32), precision=lax.Precision.HIGHEST)
    elem_count, node_count, orb_count = partial_value.shape
    face_count = one_hot.shape[1]
    partial_value = partial_value.reshape(elem_count, node_count // face_count, face_count, orb_count)
    return assemble(partial_value, one_hot).reshape(elem_count, node_count, orb_count)


def reference(orbitals, element_matrix, face_map, panel_order):
    one_hot = (face_map[:, :, None] == jnp.arange(FACE, dtype=jnp.int32)[None, None, :]).astype(jnp.float32)
    matrices = element_matrix.astype(jnp.float32)
    block_count = ORBITALS // ORB_DEV
    stacked = orbitals.reshape(ELEMENTS, NODES_EL, block_count, ORB_DEV).transpose(2, 0, 1, 3)

    def filter_block(source):
        start = source.astype(jnp.float32)
        first = ((operate(matrices, one_hot, source) - center_value * start) / half_width).astype(jnp.bfloat16)
        first_wide = first.astype(jnp.float32)
        second = 2.0 * (operate(matrices, one_hot, first) - center_value * first_wide) / half_width - start
        return second.astype(jnp.bfloat16)

    result = lax.map(filter_block, stacked)
    filtered = result.transpose(1, 2, 0, 3).reshape(ELEMENTS, NODES_EL, ORBITALS)
    flat = filtered.reshape(ELEMENTS * NODES_EL, ORBITALS)
    columns = (panel_order[:, None] * PANEL + jnp.arange(PANEL, dtype=jnp.int32)[None, :]).reshape(-1).astype(jnp.int32)
    chosen = jnp.take(flat, columns, axis=1)
    margin = lax.dot_general(flat, chosen, (((0,), (0,)), ((), ())), preferred_element_type=jnp.float32)
    margin = margin * (float(ELEMENTS * NODES_EL) ** -0.5)
    return filtered, margin
```

```python
import functools

import jax
import jax.numpy as jnp
from jax import lax
from jax.experimental import pallas as pl
from jax.experimental.pallas import tpu as pltpu
from jax.sharding import PartitionSpec as P

PANEL = 128
PANELS = 4
PARTS = 4
LAG = 3
SUBLANES = 16

center_value = 0.5
half_width = 2.0

MESH = pl.DeviceIdType.MESH


def passed_along(shard, axis, by):
    devices = lax.axis_size(axis)
    return lax.ppermute(shard, axis, [(i, (i + by) % devices) for i in range(devices)])


def operate(matrices, one_hot, values):
    partial_value = jnp.einsum("enm,emo->eno", matrices, values, preferred_element_type=jnp.float32)
    elem_count, node_count, orb_count = partial_value.shape
    face_count = one_hot.shape[1]
    partial_value = partial_value.reshape(
        elem_count, node_count // face_count, face_count, orb_count
    )
    top_face = partial_value[:, -1]
    low_face = partial_value[:, 0]
    moved_top = jnp.einsum("gfj,gfo->gjo", one_hot, top_face, precision=lax.Precision.HIGHEST)
    from_above = passed_along(low_face[0], "mesh", -1)
    upper_next = jnp.concatenate([low_face[1:], from_above[None]], 0)
    summed = top_face + jnp.einsum(
        "gfj,gjo->gfo", one_hot, upper_next, precision=lax.Precision.HIGHEST
    )
    from_below = passed_along(moved_top[-1].astype(jnp.bfloat16), "mesh", 1).astype(jnp.float32)
    lower_new = low_face + jnp.concatenate([from_below[None], moved_top[:-1]], 0)
    partial_value = partial_value.at[:, 0].set(lower_new).at[:, -1].set(summed)
    return partial_value.reshape(elem_count, node_count, orb_count)


def margin_kernel(
    n, nb, groups, scale, columns_ref, f_ref, out_ref,
    own, going_up, going_down, turned, part, arrived, gathered,
    up_send, up_recv, down_send, down_recv, rs_send, rs_recv, ag_send, ag_recv,
):
    me = lax.axis_index("mesh")
    z = lax.axis_index("band")
    rows, cols = f_ref.shape
    chunk = rows // PARTS
    total = PANELS * PARTS
    slice_rows = arrived.shape[2]
    per_group = PANELS // groups
    per_panel = n // per_group

    barrier = pltpu.get_barrier_semaphore()

    @pl.loop(1, n)
    def _(d):
        pl.semaphore_signal(
            barrier, inc=1, device_id={"mesh": lax.rem(me + d, n)}, device_id_type=MESH
        )

    @pl.when(z > 0)
    def _():
        pl.semaphore_signal(barrier, inc=1, device_id={"band": z - 1}, device_id_type=MESH)

    @pl.when(z < nb - 1)
    def _():
        pl.semaphore_signal(barrier, inc=1, device_id={"band": z + 1}, device_id_type=MESH)

    here = lax.broadcasted_iota(jnp.int32, (cols, PANELS * PANEL), 0) + z * cols
    picked = jnp.dot(
        f_ref[...],
        (here == columns_ref[...]).astype(jnp.float32).astype(jnp.bfloat16),
        preferred_element_type=jnp.float32,
    ).astype(jnp.bfloat16)
    for k in range(PANELS):
        own[k * PARTS:(k + 1) * PARTS] = picked[:, k * PANEL:(k + 1) * PANEL].reshape(
            PARTS, chunk, PANEL
        )

    @pl.when(z == 0)
    def _():
        going_up[...] = own[...]

    @pl.when(z == nb - 1)
    def _():
        going_down[...] = own[...]

    pl.semaphore_wait(barrier, n - 1 + jnp.minimum(z, 1) + jnp.minimum(nb - 1 - z, 1))

    def sweep_copy(buffer, idx, send, recv, target):
        return pltpu.make_async_remote_copy(
            src_ref=buffer.at[idx], dst_ref=buffer.at[idx],
            send_sem=send.at[idx], recv_sem=recv.at[idx],
            device_id={"band": target}, device_id_type=MESH,
        )

    def pass_on(idx, buffer, send, recv, first, last, target):
        @pl.when(jnp.logical_and(idx >= 0, idx < total))
        def _():
            @pl.when(jnp.logical_not(first))
            def _():
                sweep_copy(buffer, idx, send, recv, target).wait_recv()
                buffer[idx] = own[idx] + buffer[idx]

            @pl.when(jnp.logical_not(last))
            def _():
                sweep_copy(buffer, idx, send, recv, target).start()

    above = lax.rem(z + 1, nb)
    below = lax.rem(z + nb - 1, nb)

    def step(s):
        pass_on(s - LAG * z, going_up, up_send, up_recv, z == 0, z == nb - 1, above)
        pass_on(
            s - LAG * (nb - 1 - z), going_down, down_send, down_recv, z == nb - 1, z == 0, below
        )

    def scatter_copy(g, d):
        target = lax.rem(me + d, n)
        return pltpu.make_async_remote_copy(
            src_ref=part.at[g, target], dst_ref=arrived.at[g, d],
            send_sem=rs_send.at[g, d], recv_sem=rs_recv.at[g, d],
            device_id={"mesh": target}, device_id_type=MESH,
        )

    def gather_copy(g, d, block):
        return pltpu.make_async_remote_copy(
            src_ref=gathered.at[g, block], dst_ref=gathered.at[g, block],
            send_sem=ag_send.at[g, d], recv_sem=ag_recv.at[g, d],
            device_id={"mesh": lax.rem(me + d, n)}, device_id_type=MESH,
        )

    def scatter(g):
        @pl.loop(1, n)
        def _(d):
            scatter_copy(g, d).start()

    def reduce(g):
        @pl.loop(1, n)
        def _(d):
            scatter_copy(g, d).wait_recv()
        summed = part[g, me].astype(jnp.float32)
        if n <= SUBLANES:
            for d in range(1, n):
                summed += arrived[g, d].astype(jnp.float32)
        else:
            summed = lax.fori_loop(
                1, n, lambda d, value: value + arrived[g, d].astype(jnp.float32), summed
            )
        gathered[g, me] = (summed * scale).astype(jnp.bfloat16)

        @pl.loop(1, n)
        def _(d):
            gather_copy(g, d, me).start()

    def finish(g):
        @pl.loop(1, n)
        def _(d):
            gather_copy(g, d, lax.rem(me + n - d, n)).wait_recv()
        for p in range(per_group):
            k = g * per_group + p
            block = gathered[g, p * per_panel:(p + 1) * per_panel]
            out_ref[:, k * PANEL:(k + 1) * PANEL] = block.reshape(cols, PANEL).astype(jnp.float32)

    @pl.loop(0, LAG * (nb - 1))
    def _(s):
        step(s)

    turned[...] = f_ref[...].T
    for k in range(PANELS):
        @pl.loop(LAG * (nb - 1) + k * PARTS, LAG * (nb - 1) + (k + 1) * PARTS)
        def _(s):
            step(s)
        mine = slice(k * PARTS, (k + 1) * PARTS)
        panel = (going_up[mine] + (going_down[mine] - own[mine])).reshape(rows, PANEL)
        product = jnp.dot(turned[...], panel, preferred_element_type=jnp.float32)
        g, p = k // per_group, k % per_group
        part[g, p * per_panel:(p + 1) * per_panel] = product.astype(jnp.bfloat16).reshape(
            per_panel, slice_rows, PANEL
        )
        if p == per_group - 1:
            scatter(g)
            if g > 0:
                reduce(g - 1)
            if g > 1:
                finish(g - 2)
    reduce(groups - 1)
    if groups > 1:
        finish(groups - 2)
    finish(groups - 1)

    @pl.loop(0, total)
    def _(idx):
        @pl.when(z < nb - 1)
        def _():
            sweep_copy(going_up, idx, up_send, up_recv, above).wait_send()

        @pl.when(z > 0)
        def _():
            sweep_copy(going_down, idx, down_send, down_recv, below).wait_send()

    for g in range(groups):
        @pl.loop(1, n)
        def _(d):
            scatter_copy(g, d).wait_send()
            gather_copy(g, d, me).wait_send()


def margin_of(flat, panel_order, n, nb):
    rows, cols = flat.shape
    groups = max(1, min(PANELS, PANELS * cols // (n * SUBLANES)))
    slice_rows = PANELS * cols // (groups * n)
    total = PANELS * PARTS
    scale = float(rows * n) ** (-0.5)
    sweep = pltpu.VMEM((total, rows // PARTS, PANEL), jnp.bfloat16)
    blocks = pltpu.VMEM((groups, n, slice_rows, PANEL), jnp.bfloat16)
    columns = (
        panel_order[:, None] * PANEL + jnp.arange(PANEL, dtype=jnp.int32)[None, :]
    ).reshape(1, PANELS * PANEL)
    dma = pltpu.SemaphoreType.DMA
    return pl.pallas_call(
        functools.partial(margin_kernel, n, nb, groups, scale),
        out_shape=jax.ShapeDtypeStruct((cols, PANELS * PANEL), jnp.float32),
        in_specs=[
            pl.BlockSpec(memory_space=pltpu.VMEM),
            pl.BlockSpec(memory_space=pltpu.VMEM),
        ],
        out_specs=pl.BlockSpec(memory_space=pltpu.VMEM),
        scratch_shapes=[
            sweep, sweep, sweep, pltpu.VMEM((cols, rows), jnp.bfloat16), blocks, blocks, blocks,
            dma((total,)), dma((total,)), dma((total,)), dma((total,)),
            dma((groups, n)), dma((groups, n)), dma((groups, n)), dma((groups, n)),
        ],
        compiler_params=pltpu.CompilerParams(collective_id=0, has_side_effects=True),
    )(columns, flat)


def on_device(n, nb, orbitals, element_matrix, face_map, panel_order):
    face_count = face_map.shape[1]
    one_hot = (
        face_map[:, :, None] == jnp.arange(face_count, dtype=jnp.int32)[None, None, :]
    ).astype(jnp.float32)
    start = orbitals.astype(jnp.float32)
    first = (
        (operate(element_matrix, one_hot, orbitals) - center_value * start) / half_width
    ).astype(jnp.bfloat16)
    first_wide = first.astype(jnp.float32)
    second = (
        2.0 * (operate(element_matrix, one_hot, first) - center_value * first_wide) / half_width
        - start
    )
    filtered = second.astype(jnp.bfloat16)
    elem_count, node_count, orb_count = filtered.shape
    flat = filtered.reshape(elem_count * node_count, orb_count)
    return (filtered, margin_of(flat, panel_order, n, nb))


def solution(mesh):
    in_specs = (P("mesh", None, "band"), P("mesh", None, None), P("mesh", None), P())
    out_specs = (P("mesh", None, "band"), P("band", None))
    return jax.shard_map(
        functools.partial(on_device, mesh.shape["mesh"], mesh.shape["band"]),
        mesh=mesh, in_specs=in_specs, out_specs=out_specs, check_vma=False,
    )
```

```python
import functools

import jax
import jax.numpy as jnp
from jax import lax
from jax.experimental import pallas as pl
from jax.experimental.pallas import tpu as pltpu
from jax.sharding import PartitionSpec as P

PANEL = 128
PANELS = 4
EARLY = 2
LAG = 3
SUBLANES = 16

center_value = 0.5
half_width = 2.0

MESH = pl.DeviceIdType.MESH


def chunk_slots(parts):
    sequence = [(k, p) for k in range(EARLY) for p in range(parts - 1)]
    sequence += [(k, parts - 1) for k in range(EARLY)]
    sequence += [(k, p) for k in range(EARLY, PANELS) for p in range(parts)]
    slot = {pair: i for i, pair in enumerate(sequence)}
    return [[slot[k, p] for p in range(parts)] for k in range(PANELS)]


def filter_kernel(
    n, nb, groups, columns_ref, row_ref, col_ref, a_ref, v_ref, f_ref, out_ref,
    wide, first, ordered, low_out, top_out, low_in, top_in, face_send, face_recv,
    own, going_up, going_down, turned, part, arrived, gathered,
    up_send, up_recv, down_send, down_recv, rs_send, rs_recv, ag_send, ag_recv,
):
    me = lax.axis_index("mesh")
    z = lax.axis_index("band")
    rows, cols = v_ref.shape
    face = col_ref.shape[0]
    chunk = 2 * face
    parts = rows // chunk
    slots = chunk_slots(parts)
    total = PANELS * parts
    early = EARLY * (parts - 1)
    inner = slice(face, rows - face)
    low, top = slice(0, face), slice(rows - face, rows)
    bf16, f32 = jnp.bfloat16, jnp.float32
    slice_rows = arrived.shape[2]
    per_group = PANELS // groups
    per_panel = n // per_group

    barrier = pltpu.get_barrier_semaphore()

    @pl.loop(1, n)
    def _(d):
        pl.semaphore_signal(
            barrier, inc=1, device_id={"mesh": lax.rem(me + d, n)}, device_id_type=MESH
        )

    @pl.when(z > 0)
    def _():
        pl.semaphore_signal(barrier, inc=1, device_id={"band": z - 1}, device_id_type=MESH)

    @pl.when(z < nb - 1)
    def _():
        pl.semaphore_signal(barrier, inc=1, device_id={"band": z + 1}, device_id_type=MESH)

    def product_of(left, right):
        return jnp.dot(left, right, preferred_element_type=f32)

    positions = lax.broadcasted_iota(jnp.int32, (face, face), 1)
    to_top = (col_ref[...] == positions).astype(f32).astype(bf16)
    positions = lax.broadcasted_iota(jnp.int32, (face, face), 0)
    to_low = (row_ref[...] == positions).astype(f32).astype(bf16)
    following, previous = lax.rem(me + 1, n), lax.rem(me + n - 1, n)

    def low_copy(t):
        return pltpu.make_async_remote_copy(
            src_ref=low_out.at[t], dst_ref=low_in.at[t],
            send_sem=face_send.at[t, 0], recv_sem=face_recv.at[t, 0],
            device_id={"mesh": previous}, device_id_type=MESH,
        )

    def top_copy(t):
        return pltpu.make_async_remote_copy(
            src_ref=top_out.at[t], dst_ref=top_in.at[t],
            send_sem=face_send.at[t, 1], recv_sem=face_recv.at[t, 1],
            device_id={"mesh": following}, device_id_type=MESH,
        )

    def send_faces(t):
        low_out[t] = wide[low].astype(bf16)
        top_out[t] = product_of(to_low, wide[top].astype(bf16)).astype(bf16)
        low_copy(t).start()
        top_copy(t).start()

    def take_faces(t):
        low_copy(t).wait_recv()
        top_copy(t).wait_recv()
        wide[top] = wide[top] + product_of(to_top, low_in[t])
        wide[low] = wide[low] + top_in[t].astype(f32)

    def first_step(where):
        start = v_ref[where].astype(f32)
        first[where] = ((wide[where] - center_value * start) / half_width).astype(bf16)

    def second_step(where):
        start = v_ref[where].astype(f32)
        value = 2.0 * (wide[where] - center_value * first[where].astype(f32)) / half_width
        f_ref[where] = (value - start).astype(bf16)

    wide[...] = product_of(a_ref[...], v_ref[...])
    pl.semaphore_wait(barrier, n - 1 + jnp.minimum(z, 1) + jnp.minimum(nb - 1 - z, 1))

    send_faces(0)
    first_step(inner)
    here = lax.broadcasted_iota(jnp.int32, (cols, PANELS * PANEL), 0) + z * cols
    picker = (here == columns_ref[...]).astype(f32).astype(bf16)
    middle = slice(chunk, rows - chunk)
    left, right = slice(0, chunk), slice(rows - chunk, rows)
    so_far = product_of(a_ref[:, middle], first[middle])
    take_faces(0)
    first_step(low)
    first_step(top)
    wide[...] = (
        so_far
        + product_of(a_ref[:, left], first[left])
        + product_of(a_ref[:, right], first[right])
    )
    send_faces(1)
    second_step(inner)

    def own_chunks(which, values):
        picked = product_of(values, picker).astype(bf16)
        for k in range(PANELS):
            for i, p in enumerate(which):
                piece = picked[i * chunk:(i + 1) * chunk, k * PANEL:(k + 1) * PANEL]
                own[slots[k][p]] = piece

        @pl.when(z == 0)
        def _():
            for k in range(PANELS):
                for p in which:
                    going_up[slots[k][p]] = own[slots[k][p]]

        @pl.when(z == nb - 1)
        def _():
            for k in range(PANELS):
                for p in which:
                    going_down[slots[k][p]] = own[slots[k][p]]

    ordered[0:rows - chunk] = f_ref[inner]
    own_chunks(list(range(parts - 1)), ordered[0:rows - chunk])

    def sweep_copy(buffer, idx, send, recv, target):
        return pltpu.make_async_remote_copy(
            src_ref=buffer.at[idx], dst_ref=buffer.at[idx],
            send_sem=send.at[idx], recv_sem=recv.at[idx],
            device_id={"band": target}, device_id_type=MESH,
        )

    def pass_on(idx, buffer, send, recv, first, last, target):
        @pl.when(jnp.logical_and(idx >= 0, idx < total))
        def _():
            @pl.when(jnp.logical_not(first))
            def _():
                sweep_copy(buffer, idx, send, recv, target).wait_recv()
                buffer[idx] = own[idx] + buffer[idx]

            @pl.when(jnp.logical_not(last))
            def _():
                sweep_copy(buffer, idx, send, recv, target).start()

    above = lax.rem(z + 1, nb)
    below = lax.rem(z + nb - 1, nb)

    def step(s):
        pass_on(s - LAG * z, going_up, up_send, up_recv, z == 0, z == nb - 1, above)
        pass_on(
            s - LAG * (nb - 1 - z), going_down, down_send, down_recv, z == nb - 1, z == 0, below
        )

    def scatter_copy(g, d):
        target = lax.rem(me + d, n)
        return pltpu.make_async_remote_copy(
            src_ref=part.at[g, target], dst_ref=arrived.at[g, d],
            send_sem=rs_send.at[g, d], recv_sem=rs_recv.at[g, d],
            device_id={"mesh": target}, device_id_type=MESH,
        )

    def gather_copy(g, d, block):
        return pltpu.make_async_remote_copy(
            src_ref=gathered.at[g, block], dst_ref=gathered.at[g, block],
            send_sem=ag_send.at[g, d], recv_sem=ag_recv.at[g, d],
            device_id={"mesh": lax.rem(me + d, n)}, device_id_type=MESH,
        )

    def scatter(g):
        @pl.loop(1, n)
        def _(d):
            scatter_copy(g, d).start()

    def reduce(g):
        @pl.loop(1, n)
        def _(d):
            scatter_copy(g, d).wait_recv()
        summed = part[g, me].astype(jnp.float32)
        if n <= SUBLANES:
            for d in range(1, n):
                summed += arrived[g, d].astype(jnp.float32)
        else:
            summed = lax.fori_loop(
                1, n, lambda d, value: value + arrived[g, d].astype(jnp.float32), summed
            )
        gathered[g, me] = (summed).astype(jnp.bfloat16)

        @pl.loop(1, n)
        def _(d):
            gather_copy(g, d, me).start()

    def finish(g):
        @pl.loop(1, n)
        def _(d):
            gather_copy(g, d, lax.rem(me + n - d, n)).wait_recv()
        for p in range(per_group):
            k = g * per_group + p
            block = gathered[g, p * per_panel:(p + 1) * per_panel]
            out_ref[:, k * PANEL:(k + 1) * PANEL] = block.reshape(cols, PANEL)

    done = early

    @pl.loop(0, early)
    def _(s):
        step(s)

    take_faces(1)
    second_step(low)
    second_step(top)
    ordered[rows - chunk:rows - face] = f_ref[low]
    ordered[rows - face:rows] = f_ref[top]
    own_chunks([parts - 1], ordered[rows - chunk:rows])
    turned[...] = ordered[...].T
    for k in range(PANELS):
        until = max(done, LAG * (nb - 1) + slots[k][-1] + 1)

        @pl.loop(done, until)
        def _(s):
            step(s)
        done = until
        panel = jnp.concatenate(
            [going_up[i] + (going_down[i] - own[i]) for i in slots[k]], 0
        )
        product = jnp.dot(turned[...], panel, preferred_element_type=jnp.float32)
        g, p = k // per_group, k % per_group
        part[g, p * per_panel:(p + 1) * per_panel] = product.astype(jnp.bfloat16).reshape(
            per_panel, slice_rows, PANEL
        )
        if p == per_group - 1:
            scatter(g)
            if g > 0:
                reduce(g - 1)
            if g > 1:
                finish(g - 2)
    reduce(groups - 1)
    if groups > 1:
        finish(groups - 2)
    finish(groups - 1)

    @pl.loop(0, total)
    def _(idx):
        @pl.when(z < nb - 1)
        def _():
            sweep_copy(going_up, idx, up_send, up_recv, above).wait_send()

        @pl.when(z > 0)
        def _():
            sweep_copy(going_down, idx, down_send, down_recv, below).wait_send()

    for t in range(2):
        low_copy(t).wait_send()
        top_copy(t).wait_send()
    for g in range(groups):
        @pl.loop(1, n)
        def _(d):
            scatter_copy(g, d).wait_send()
            gather_copy(g, d, me).wait_send()


def on_device(n, nb, orbitals, element_matrix, face_map, panel_order):
    elements, rows, cols = orbitals.shape
    face = face_map.shape[1]
    groups = max(1, min(PANELS, PANELS * cols // (n * SUBLANES)))
    slice_rows = PANELS * cols // (groups * n)
    chunk = 2 * face
    total = PANELS * rows // chunk
    scale = float(rows * n) ** (-0.5)
    bf16 = jnp.bfloat16
    sweep = pltpu.VMEM((total, chunk, PANEL), bf16)
    blocks = pltpu.VMEM((groups, n, slice_rows, PANEL), bf16)
    faces = pltpu.VMEM((2, face, cols), bf16)
    square = pltpu.VMEM((rows, cols), bf16)
    dma = pltpu.SemaphoreType.DMA
    columns = (
        panel_order[:, None] * PANEL + jnp.arange(PANEL, dtype=jnp.int32)[None, :]
    ).reshape(1, PANELS * PANEL)
    filtered, margin = pl.pallas_call(
        functools.partial(filter_kernel, n, nb, groups),
        out_shape=(
            jax.ShapeDtypeStruct((rows, cols), bf16),
            jax.ShapeDtypeStruct((cols, PANELS * PANEL), bf16),
        ),
        in_specs=[pl.BlockSpec(memory_space=pltpu.VMEM)] * 5,
        out_specs=(pl.BlockSpec(memory_space=pltpu.VMEM),) * 2,
        scratch_shapes=[
            pltpu.VMEM((rows, cols), jnp.float32), square, square,
            faces, faces, faces, faces, dma((2, 2)), dma((2, 2)),
            sweep, sweep, sweep, pltpu.VMEM((cols, rows), bf16), blocks, blocks, blocks,
            dma((total,)), dma((total,)), dma((total,)), dma((total,)),
            dma((groups, n)), dma((groups, n)), dma((groups, n)), dma((groups, n)),
        ],
        compiler_params=pltpu.CompilerParams(collective_id=0, has_side_effects=True),
    )(
        columns, face_map, face_map.reshape(face, 1),
        element_matrix.reshape(rows, rows), orbitals.reshape(rows, cols),
    )
    return (filtered.reshape(elements, rows, cols), margin.astype(jnp.float32) * scale)


def solution(mesh):
    in_specs = (P("mesh", None, "band"), P("mesh", None, None), P("mesh", None), P())
    out_specs = (P("mesh", None, "band"), P("band", None))
    return jax.shard_map(
        functools.partial(on_device, mesh.shape["mesh"], mesh.shape["band"]),
        mesh=mesh, in_specs=in_specs, out_specs=out_specs, check_vma=False,
    )
```

```python
import functools

import jax
import jax.numpy as jnp
from jax import lax
from jax.experimental import pallas as pl
from jax.experimental.pallas import tpu as pltpu
from jax.sharding import PartitionSpec as P

PANEL = 128
PANELS = 4
EARLY = 2
LAG = 5
SUBLANES = 16

center_value = 0.5
half_width = 2.0

MESH = pl.DeviceIdType.MESH


def chunk_slots(parts):
    sequence = [(k, p) for k in range(EARLY) for p in range(parts - 1)]
    sequence += [(k, parts - 1) for k in range(EARLY)]
    sequence += [(k, p) for k in range(EARLY, PANELS) for p in range(parts)]
    slot = {pair: i for i, pair in enumerate(sequence)}
    return [[slot[k, p] for p in range(parts)] for k in range(PANELS)]


def filter_kernel(
    n, nb, groups, order_ref, row_ref, a_ref, v_ref, f_ref, out_ref,
    wide, first, ordered, low_out, top_out, low_in, top_in, face_send, face_recv,
    own, going_up, going_down, turned, part, arrived, gathered,
    up_send, up_recv, down_send, down_recv, rs_send, rs_recv, ag_send, ag_recv,
):
    me = lax.axis_index("mesh")
    z = lax.axis_index("band")
    rows, cols = v_ref.shape
    face = row_ref.shape[1]
    chunk = 2 * face
    parts = rows // chunk
    slots = chunk_slots(parts)
    total = PANELS * parts
    early = EARLY * (parts - 1)
    inner = slice(face, rows - face)
    low, top = slice(0, face), slice(rows - face, rows)
    bf16, f32 = jnp.bfloat16, jnp.float32
    slice_rows = arrived.shape[2]
    per_group = PANELS // groups
    per_panel = n // per_group

    barrier = pltpu.get_barrier_semaphore()

    @pl.loop(1, n)
    def _(d):
        pl.semaphore_signal(
            barrier, inc=1, device_id={"mesh": lax.rem(me + d, n)}, device_id_type=MESH
        )

    @pl.when(z > 0)
    def _():
        pl.semaphore_signal(barrier, inc=1, device_id={"band": z - 1}, device_id_type=MESH)

    @pl.when(z < nb - 1)
    def _():
        pl.semaphore_signal(barrier, inc=1, device_id={"band": z + 1}, device_id_type=MESH)

    def product_of(left, right):
        return jnp.dot(left, right, preferred_element_type=f32)

    positions = lax.broadcasted_iota(jnp.int32, (face, face), 0)
    one_hot = (row_ref[...] == positions).astype(f32)
    to_low, to_top = one_hot.astype(bf16), one_hot.T.astype(bf16)
    following, previous = lax.rem(me + 1, n), lax.rem(me + n - 1, n)

    def low_copy(t):
        return pltpu.make_async_remote_copy(
            src_ref=low_out.at[t], dst_ref=low_in.at[t],
            send_sem=face_send.at[t, 0], recv_sem=face_recv.at[t, 0],
            device_id={"mesh": previous}, device_id_type=MESH,
        )

    def top_copy(t):
        return pltpu.make_async_remote_copy(
            src_ref=top_out.at[t], dst_ref=top_in.at[t],
            send_sem=face_send.at[t, 1], recv_sem=face_recv.at[t, 1],
            device_id={"mesh": following}, device_id_type=MESH,
        )

    def send_faces(t):
        low_out[t] = wide[low].astype(bf16)
        top_out[t] = product_of(to_low, wide[top].astype(bf16)).astype(bf16)
        low_copy(t).start()
        top_copy(t).start()

    def take_faces(t):
        low_copy(t).wait_recv()
        top_copy(t).wait_recv()
        wide[top] = wide[top] + product_of(to_top, low_in[t])
        wide[low] = wide[low] + top_in[t].astype(f32)

    def first_step(where):
        start = v_ref[where].astype(f32)
        first[where] = ((wide[where] - center_value * start) / half_width).astype(bf16)

    def second_step(where):
        start = v_ref[where].astype(f32)
        value = 2.0 * (wide[where] - center_value * first[where].astype(f32)) / half_width
        f_ref[where] = (value - start).astype(bf16)

    both = product_of(jnp.concatenate([a_ref[low], a_ref[top]], 0), v_ref[...])
    wide[low], wide[top] = both[:face], both[face:]
    pl.semaphore_wait(barrier, n - 1 + jnp.minimum(z, 1) + jnp.minimum(nb - 1 - z, 1))

    send_faces(0)
    wide[inner] = product_of(a_ref[inner], v_ref[...])
    first_step(inner)
    here = lax.broadcasted_iota(jnp.int32, (cols, PANEL), 0) + z * cols
    here = here - lax.broadcasted_iota(jnp.int32, (cols, PANEL), 1)
    picker = jnp.concatenate(
        [(here == order_ref[k] * PANEL).astype(f32).astype(bf16) for k in range(PANELS)], 1
    )
    middle = slice(chunk, rows - chunk)
    left, right = slice(0, chunk), slice(rows - chunk, rows)
    so_far = product_of(a_ref[:, middle], first[middle])
    take_faces(0)
    first_step(low)
    first_step(top)
    outer_left = jnp.concatenate([a_ref[:, left], a_ref[:, right]], 1)
    outer_right = jnp.concatenate([first[left], first[right]], 0)
    both = product_of(
        jnp.concatenate([outer_left[low], outer_left[top]], 0), outer_right
    )
    wide[low], wide[top] = so_far[low] + both[:face], so_far[top] + both[face:]
    send_faces(1)
    wide[inner] = so_far[inner] + product_of(outer_left[inner], outer_right)
    second_step(inner)

    def own_chunks(which, values):
        picked = product_of(values, picker).astype(bf16)
        for k in range(PANELS):
            for i, p in enumerate(which):
                piece = picked[i * chunk:(i + 1) * chunk, k * PANEL:(k + 1) * PANEL]
                own[slots[k][p]] = piece

        @pl.when(z == 0)
        def _():
            for k in range(PANELS):
                for p in which:
                    going_up[slots[k][p]] = own[slots[k][p]]

        @pl.when(z == nb - 1)
        def _():
            for k in range(PANELS):
                for p in which:
                    going_down[slots[k][p]] = own[slots[k][p]]

    ordered[0:rows - chunk] = f_ref[inner]
    own_chunks(list(range(parts - 1)), ordered[0:rows - chunk])

    def sweep_copy(buffer, idx, send, recv, target):
        return pltpu.make_async_remote_copy(
            src_ref=buffer.at[idx], dst_ref=buffer.at[idx],
            send_sem=send.at[idx], recv_sem=recv.at[idx],
            device_id={"band": target}, device_id_type=MESH,
        )

    def pass_on(idx, buffer, send, recv, first, last, target):
        @pl.when(jnp.logical_and(idx >= 0, idx < total))
        def _():
            @pl.when(jnp.logical_not(first))
            def _():
                sweep_copy(buffer, idx, send, recv, target).wait_recv()
                buffer[idx] = own[idx] + buffer[idx]

            @pl.when(jnp.logical_not(last))
            def _():
                sweep_copy(buffer, idx, send, recv, target).start()

    above = lax.rem(z + 1, nb)
    below = lax.rem(z + nb - 1, nb)

    def step(s):
        pass_on(s - LAG * z, going_up, up_send, up_recv, z == 0, z == nb - 1, above)
        pass_on(
            s - LAG * (nb - 1 - z), going_down, down_send, down_recv, z == nb - 1, z == 0, below
        )

    def scatter_copy(g, d):
        target = lax.rem(me + d, n)
        return pltpu.make_async_remote_copy(
            src_ref=part.at[g, target], dst_ref=arrived.at[g, d],
            send_sem=rs_send.at[g, d], recv_sem=rs_recv.at[g, d],
            device_id={"mesh": target}, device_id_type=MESH,
        )

    def gather_copy(g, d, block):
        return pltpu.make_async_remote_copy(
            src_ref=gathered.at[g, block], dst_ref=gathered.at[g, block],
            send_sem=ag_send.at[g, d], recv_sem=ag_recv.at[g, d],
            device_id={"mesh": lax.rem(me + d, n)}, device_id_type=MESH,
        )

    def scatter(g):
        @pl.loop(1, n)
        def _(d):
            scatter_copy(g, d).start()

    def reduce(g):
        @pl.loop(1, n)
        def _(d):
            scatter_copy(g, d).wait_recv()
        summed = part[g, me].astype(jnp.float32)
        if n <= SUBLANES:
            for d in range(1, n):
                summed += arrived[g, d].astype(jnp.float32)
        else:
            summed = lax.fori_loop(
                1, n, lambda d, value: value + arrived[g, d].astype(jnp.float32), summed
            )
        gathered[g, me] = (summed).astype(jnp.bfloat16)

        @pl.loop(1, n)
        def _(d):
            gather_copy(g, d, me).start()

    def finish(g):
        @pl.loop(1, n)
        def _(d):
            gather_copy(g, d, lax.rem(me + n - d, n)).wait_recv()
        for p in range(per_group):
            k = g * per_group + p
            block = gathered[g, p * per_panel:(p + 1) * per_panel]
            out_ref[:, k * PANEL:(k + 1) * PANEL] = block.reshape(cols, PANEL)

    done = early

    @pl.loop(0, early)
    def _(s):
        step(s)

    take_faces(1)
    second_step(low)
    second_step(top)
    ordered[rows - chunk:rows - face] = f_ref[low]
    ordered[rows - face:rows] = f_ref[top]
    own_chunks([parts - 1], ordered[rows - chunk:rows])
    turned[...] = ordered[...].T
    for k in range(PANELS):
        until = max(done, LAG * (nb - 1) + slots[k][-1] + 1)

        @pl.loop(done, until)
        def _(s):
            step(s)
        done = until
        panel = jnp.concatenate(
            [going_up[i] + (going_down[i] - own[i]) for i in slots[k]], 0
        )
        product = jnp.dot(turned[...], panel, preferred_element_type=jnp.float32)
        g, p = k // per_group, k % per_group
        part[g, p * per_panel:(p + 1) * per_panel] = product.astype(jnp.bfloat16).reshape(
            per_panel, slice_rows, PANEL
        )
        if p == per_group - 1:
            scatter(g)
            if g > 1:
                reduce(g - 2)
    for g in range(max(groups - 2, 0), groups):
        reduce(g)
    for g in range(groups):
        finish(g)

    @pl.loop(0, total)
    def _(idx):
        @pl.when(z < nb - 1)
        def _():
            sweep_copy(going_up, idx, up_send, up_recv, above).wait_send()

        @pl.when(z > 0)
        def _():
            sweep_copy(going_down, idx, down_send, down_recv, below).wait_send()

    for t in range(2):
        low_copy(t).wait_send()
        top_copy(t).wait_send()
    for g in range(groups):
        @pl.loop(1, n)
        def _(d):
            scatter_copy(g, d).wait_send()
            gather_copy(g, d, me).wait_send()


def write_kernel(scale, f_ref, m_ref, filtered_ref, margin_ref):
    filtered_ref[...] = f_ref[...]
    margin_ref[...] = m_ref[...].astype(jnp.float32) * scale


def on_device(n, nb, orbitals, element_matrix, face_map, panel_order):
    elements, rows, cols = orbitals.shape
    face = face_map.shape[1]
    groups = max(1, min(PANELS, PANELS * cols // (n * SUBLANES)))
    slice_rows = PANELS * cols // (groups * n)
    chunk = 2 * face
    total = PANELS * rows // chunk
    scale = float(rows * n) ** (-0.5)
    bf16 = jnp.bfloat16
    sweep = pltpu.VMEM((total, chunk, PANEL), bf16)
    blocks = pltpu.VMEM((groups, n, slice_rows, PANEL), bf16)
    faces = pltpu.VMEM((2, face, cols), bf16)
    square = pltpu.VMEM((rows, cols), bf16)
    dma = pltpu.SemaphoreType.DMA
    filtered, margin = pl.pallas_call(
        functools.partial(filter_kernel, n, nb, groups),
        out_shape=(
            jax.ShapeDtypeStruct((rows, cols), bf16),
            jax.ShapeDtypeStruct((cols, PANELS * PANEL), bf16),
        ),
        in_specs=[pl.BlockSpec(memory_space=pltpu.SMEM)]
        + [pl.BlockSpec(memory_space=pltpu.VMEM)] * 3,
        out_specs=(pl.BlockSpec(memory_space=pltpu.VMEM),) * 2,
        scratch_shapes=[
            pltpu.VMEM((rows, cols), jnp.float32), square, square,
            faces, faces, faces, faces, dma((2, 2)), dma((2, 2)),
            sweep, sweep, sweep, pltpu.VMEM((cols, rows), bf16), blocks, blocks, blocks,
            dma((total,)), dma((total,)), dma((total,)), dma((total,)),
            dma((groups, n)), dma((groups, n)), dma((groups, n)), dma((groups, n)),
        ],
        compiler_params=pltpu.CompilerParams(collective_id=0, has_side_effects=True),
    )(
        panel_order, face_map,
        element_matrix.reshape(rows, rows), orbitals.reshape(rows, cols),
    )
    steps = 1
    narrow = pl.BlockSpec((rows // steps, cols), lambda i: (i, 0))
    wide = pl.BlockSpec((cols // steps, PANELS * PANEL), lambda i: (i, 0))
    filtered, margin = pl.pallas_call(
        functools.partial(write_kernel, scale),
        grid=(steps,),
        out_shape=(
            jax.ShapeDtypeStruct((rows, cols), bf16),
            jax.ShapeDtypeStruct((cols, PANELS * PANEL), jnp.float32),
        ),
        in_specs=[narrow, wide],
        out_specs=(narrow, wide),
    )(filtered, margin)
    return (filtered.reshape(elements, rows, cols), margin)


def solution(mesh):
    in_specs = (P("mesh", None, "band"), P("mesh", None, None), P("mesh", None), P())
    out_specs = (P("mesh", None, "band"), P("band", None))
    return jax.shard_map(
        functools.partial(on_device, mesh.shape["mesh"], mesh.shape["band"]),
        mesh=mesh, in_specs=in_specs, out_specs=out_specs, check_vma=False,
    )
```

```python
import functools

import jax
import jax.numpy as jnp
from jax import lax
from jax.experimental import pallas as pl
from jax.experimental.pallas import tpu as pltpu
from jax.sharding import PartitionSpec as P

PANEL = 128
PANELS = 4
EARLY = 2
LAG = 5
SUBLANES = 16

center_value = 0.5
half_width = 2.0

MESH = pl.DeviceIdType.MESH


def chunk_slots(parts):
    sequence = [(k, p) for k in range(EARLY) for p in range(parts - 1)]
    sequence += [(k, parts - 1) for k in range(EARLY)]
    sequence += [(k, p) for k in range(EARLY, PANELS) for p in range(parts)]
    slot = {pair: i for i, pair in enumerate(sequence)}
    return [[slot[k, p] for p in range(parts)] for k in range(PANELS)]


def filter_kernel(
    n, nb, groups, order_ref, row_ref, a_hbm, v_hbm, f_hbm, out_ref,
    a_ref, v_ref, f_ref, local, wide, first, ordered, low_out, top_out, low_in, top_in, face_send, face_recv,
    own, going_up, going_down, turned, part, arrived, gathered,
    up_send, up_recv, down_send, down_recv, rs_send, rs_recv, ag_send, ag_recv,
):
    me = lax.axis_index("mesh")
    z = lax.axis_index("band")
    rows, cols = v_ref.shape
    face = row_ref.shape[1]
    chunk = 2 * face
    parts = rows // chunk
    slots = chunk_slots(parts)
    total = PANELS * parts
    early = EARLY * (parts - 1)
    inner = slice(face, rows - face)
    low, top = slice(0, face), slice(rows - face, rows)
    bf16, f32 = jnp.bfloat16, jnp.float32
    slice_rows = arrived.shape[2]
    per_group = PANELS // groups
    per_panel = n // per_group

    load_a = pltpu.make_async_copy(a_hbm, a_ref, local.at[0])
    load_v = pltpu.make_async_copy(v_hbm, v_ref, local.at[1])
    store_f = pltpu.make_async_copy(f_ref, f_hbm, local.at[2])
    load_a.start()
    load_v.start()
    barrier = pltpu.get_barrier_semaphore()

    @pl.loop(1, n)
    def _(d):
        pl.semaphore_signal(
            barrier, inc=1, device_id={"mesh": lax.rem(me + d, n)}, device_id_type=MESH
        )

    @pl.when(z > 0)
    def _():
        pl.semaphore_signal(barrier, inc=1, device_id={"band": z - 1}, device_id_type=MESH)

    @pl.when(z < nb - 1)
    def _():
        pl.semaphore_signal(barrier, inc=1, device_id={"band": z + 1}, device_id_type=MESH)

    def product_of(left, right):
        return jnp.dot(left, right, preferred_element_type=f32)

    positions = lax.broadcasted_iota(jnp.int32, (face, face), 0)
    one_hot = (row_ref[...] == positions).astype(f32)
    to_low, to_top = one_hot.astype(bf16), one_hot.T.astype(bf16)
    following, previous = lax.rem(me + 1, n), lax.rem(me + n - 1, n)

    def low_copy(t):
        return pltpu.make_async_remote_copy(
            src_ref=low_out.at[t], dst_ref=low_in.at[t],
            send_sem=face_send.at[t, 0], recv_sem=face_recv.at[t, 0],
            device_id={"mesh": previous}, device_id_type=MESH,
        )

    def top_copy(t):
        return pltpu.make_async_remote_copy(
            src_ref=top_out.at[t], dst_ref=top_in.at[t],
            send_sem=face_send.at[t, 1], recv_sem=face_recv.at[t, 1],
            device_id={"mesh": following}, device_id_type=MESH,
        )

    def send_faces(t):
        low_out[t] = wide[low].astype(bf16)
        top_out[t] = product_of(to_low, wide[top].astype(bf16)).astype(bf16)
        low_copy(t).start()
        top_copy(t).start()

    def take_faces(t):
        low_copy(t).wait_recv()
        top_copy(t).wait_recv()
        wide[top] = wide[top] + product_of(to_top, low_in[t])
        wide[low] = wide[low] + top_in[t].astype(f32)

    def first_step(where):
        start = v_ref[where].astype(f32)
        first[where] = ((wide[where] - center_value * start) / half_width).astype(bf16)

    def second_step(where):
        start = v_ref[where].astype(f32)
        value = 2.0 * (wide[where] - center_value * first[where].astype(f32)) / half_width
        f_ref[where] = (value - start).astype(bf16)

    here = lax.broadcasted_iota(jnp.int32, (cols, PANEL), 0) + z * cols
    here = here - lax.broadcasted_iota(jnp.int32, (cols, PANEL), 1)
    picker = jnp.concatenate(
        [(here == order_ref[k] * PANEL).astype(f32).astype(bf16) for k in range(PANELS)], 1
    )
    load_a.wait()
    load_v.wait()
    both = product_of(jnp.concatenate([a_ref[low], a_ref[top]], 0), v_ref[...])
    wide[low], wide[top] = both[:face], both[face:]
    pl.semaphore_wait(barrier, n - 1 + jnp.minimum(z, 1) + jnp.minimum(nb - 1 - z, 1))

    send_faces(0)
    wide[inner] = product_of(a_ref[inner], v_ref[...])
    first_step(inner)
    middle = slice(chunk, rows - chunk)
    left, right = slice(0, chunk), slice(rows - chunk, rows)
    so_far = product_of(a_ref[:, middle], first[middle])
    take_faces(0)
    first_step(low)
    first_step(top)
    outer_left = jnp.concatenate([a_ref[:, left], a_ref[:, right]], 1)
    outer_right = jnp.concatenate([first[left], first[right]], 0)
    both = product_of(
        jnp.concatenate([outer_left[low], outer_left[top]], 0), outer_right
    )
    wide[low], wide[top] = so_far[low] + both[:face], so_far[top] + both[face:]
    send_faces(1)
    wide[inner] = so_far[inner] + product_of(outer_left[inner], outer_right)
    second_step(inner)

    def own_chunks(which, values):
        picked = product_of(values, picker).astype(bf16)
        for k in range(PANELS):
            for i, p in enumerate(which):
                piece = picked[i * chunk:(i + 1) * chunk, k * PANEL:(k + 1) * PANEL]
                own[slots[k][p]] = piece

        @pl.when(z == 0)
        def _():
            for k in range(PANELS):
                for p in which:
                    going_up[slots[k][p]] = own[slots[k][p]]

        @pl.when(z == nb - 1)
        def _():
            for k in range(PANELS):
                for p in which:
                    going_down[slots[k][p]] = own[slots[k][p]]

    ordered[0:rows - chunk] = f_ref[inner]
    own_chunks(list(range(parts - 1)), ordered[0:rows - chunk])

    def sweep_copy(buffer, idx, send, recv, target):
        return pltpu.make_async_remote_copy(
            src_ref=buffer.at[idx], dst_ref=buffer.at[idx],
            send_sem=send.at[idx], recv_sem=recv.at[idx],
            device_id={"band": target}, device_id_type=MESH,
        )

    def pass_on(idx, buffer, send, recv, first, last, target):
        @pl.when(jnp.logical_and(idx >= 0, idx < total))
        def _():
            @pl.when(jnp.logical_not(first))
            def _():
                sweep_copy(buffer, idx, send, recv, target).wait_recv()
                buffer[idx] = own[idx] + buffer[idx]

            @pl.when(jnp.logical_not(last))
            def _():
                sweep_copy(buffer, idx, send, recv, target).start()

    above = lax.rem(z + 1, nb)
    below = lax.rem(z + nb - 1, nb)

    def step(s):
        pass_on(s - LAG * z, going_up, up_send, up_recv, z == 0, z == nb - 1, above)
        pass_on(
            s - LAG * (nb - 1 - z), going_down, down_send, down_recv, z == nb - 1, z == 0, below
        )

    def scatter_copy(g, d):
        target = lax.rem(me + d, n)
        return pltpu.make_async_remote_copy(
            src_ref=part.at[g, target], dst_ref=arrived.at[g, d],
            send_sem=rs_send.at[g, d], recv_sem=rs_recv.at[g, d],
            device_id={"mesh": target}, device_id_type=MESH,
        )

    def gather_copy(g, d, block):
        return pltpu.make_async_remote_copy(
            src_ref=gathered.at[g, block], dst_ref=gathered.at[g, block],
            send_sem=ag_send.at[g, d], recv_sem=ag_recv.at[g, d],
            device_id={"mesh": lax.rem(me + d, n)}, device_id_type=MESH,
        )

    def scatter(g):
        @pl.loop(1, n)
        def _(d):
            scatter_copy(g, d).start()

    def reduce(g):
        @pl.loop(1, n)
        def _(d):
            scatter_copy(g, d).wait_recv()
        summed = part[g, me].astype(jnp.float32)
        if n <= SUBLANES:
            for d in range(1, n):
                summed += arrived[g, d].astype(jnp.float32)
        else:
            summed = lax.fori_loop(
                1, n, lambda d, value: value + arrived[g, d].astype(jnp.float32), summed
            )
        gathered[g, me] = (summed).astype(jnp.bfloat16)

        @pl.loop(1, n)
        def _(d):
            gather_copy(g, d, me).start()

    def finish(g):
        @pl.loop(1, n)
        def _(d):
            gather_copy(g, d, lax.rem(me + n - d, n)).wait_recv()
        for p in range(per_group):
            k = g * per_group + p
            block = gathered[g, p * per_panel:(p + 1) * per_panel]
            out_ref[:, k * PANEL:(k + 1) * PANEL] = block.reshape(cols, PANEL)

    done = early

    @pl.loop(0, early)
    def _(s):
        step(s)

    take_faces(1)
    second_step(low)
    second_step(top)
    store_f.start()
    ordered[rows - chunk:rows - face] = f_ref[low]
    ordered[rows - face:rows] = f_ref[top]
    own_chunks([parts - 1], ordered[rows - chunk:rows])
    turned[...] = ordered[...].T
    for k in range(PANELS):
        until = max(done, LAG * (nb - 1) + slots[k][-1] + 1)

        @pl.loop(done, until)
        def _(s):
            step(s)
        done = until
        panel = jnp.concatenate(
            [going_up[i] + (going_down[i] - own[i]) for i in slots[k]], 0
        )
        product = jnp.dot(turned[...], panel, preferred_element_type=jnp.float32)
        g, p = k // per_group, k % per_group
        part[g, p * per_panel:(p + 1) * per_panel] = product.astype(jnp.bfloat16).reshape(
            per_panel, slice_rows, PANEL
        )
        if p == per_group - 1:
            scatter(g)
            if g > 1:
                reduce(g - 2)
    for g in range(max(groups - 2, 0), groups):
        reduce(g)
    for g in range(groups):
        finish(g)

    @pl.loop(0, total)
    def _(idx):
        @pl.when(z < nb - 1)
        def _():
            sweep_copy(going_up, idx, up_send, up_recv, above).wait_send()

        @pl.when(z > 0)
        def _():
            sweep_copy(going_down, idx, down_send, down_recv, below).wait_send()

    store_f.wait()
    for t in range(2):
        low_copy(t).wait_send()
        top_copy(t).wait_send()
    for g in range(groups):
        @pl.loop(1, n)
        def _(d):
            scatter_copy(g, d).wait_send()
            gather_copy(g, d, me).wait_send()


def write_kernel(scale, f_ref, m_ref, filtered_ref, margin_ref):
    filtered_ref[...] = f_ref[...]
    margin_ref[...] = m_ref[...].astype(jnp.float32) * scale


def on_device(n, nb, orbitals, element_matrix, face_map, panel_order):
    elements, rows, cols = orbitals.shape
    face = face_map.shape[1]
    groups = max(1, min(PANELS, PANELS * cols // (n * SUBLANES)))
    slice_rows = PANELS * cols // (groups * n)
    chunk = 2 * face
    total = PANELS * rows // chunk
    scale = float(rows * n) ** (-0.5)
    bf16 = jnp.bfloat16
    sweep = pltpu.VMEM((total, chunk, PANEL), bf16)
    blocks = pltpu.VMEM((groups, n, slice_rows, PANEL), bf16)
    faces = pltpu.VMEM((2, face, cols), bf16)
    square = pltpu.VMEM((rows, cols), bf16)
    dma = pltpu.SemaphoreType.DMA
    filtered, margin = pl.pallas_call(
        functools.partial(filter_kernel, n, nb, groups),
        out_shape=(
            jax.ShapeDtypeStruct((rows, cols), bf16),
            jax.ShapeDtypeStruct((cols, PANELS * PANEL), bf16),
        ),
        in_specs=[pl.BlockSpec(memory_space=pltpu.SMEM)]
        + [pl.BlockSpec(memory_space=pltpu.VMEM)]
        + [pl.BlockSpec(memory_space=pl.ANY)] * 2,
        out_specs=(
            pl.BlockSpec(memory_space=pl.ANY), pl.BlockSpec(memory_space=pltpu.VMEM)
        ),
        scratch_shapes=[
            pltpu.VMEM((rows, rows), bf16), square, square, dma((3,)),
            pltpu.VMEM((rows, cols), jnp.float32), square, square,
            faces, faces, faces, faces, dma((2, 2)), dma((2, 2)),
            sweep, sweep, sweep, pltpu.VMEM((cols, rows), bf16), blocks, blocks, blocks,
            dma((total,)), dma((total,)), dma((total,)), dma((total,)),
            dma((groups, n)), dma((groups, n)), dma((groups, n)), dma((groups, n)),
        ],
        compiler_params=pltpu.CompilerParams(collective_id=0, has_side_effects=True),
    )(
        panel_order, face_map,
        element_matrix.reshape(rows, rows), orbitals.reshape(rows, cols),
    )
    steps = 1
    narrow = pl.BlockSpec((rows // steps, cols), lambda i: (i, 0))
    wide = pl.BlockSpec((cols // steps, PANELS * PANEL), lambda i: (i, 0))
    filtered, margin = pl.pallas_call(
        functools.partial(write_kernel, scale),
        grid=(steps,),
        out_shape=(
            jax.ShapeDtypeStruct((rows, cols), bf16),
            jax.ShapeDtypeStruct((cols, PANELS * PANEL), jnp.float32),
        ),
        in_specs=[narrow, wide],
        out_specs=(narrow, wide),
    )(filtered, margin)
    return (filtered.reshape(elements, rows, cols), margin)


def solution(mesh):
    in_specs = (P("mesh", None, "band"), P("mesh", None, None), P("mesh", None), P())
    out_specs = (P("mesh", None, "band"), P("band", None))
    return jax.shard_map(
        functools.partial(on_device, mesh.shape["mesh"], mesh.shape["band"]),
        mesh=mesh, in_specs=in_specs, out_specs=out_specs, check_vma=False,
    )
```
